32 devices in a mesh: row: 4 (over y, x), col: 8 (over z, core).
Axes of the slice: x: 2, y: 2, z: 4, core: 2. Of those that a mesh axis runs over, the one named last changes fastest.
Arguments:
- features: float32 [2048, 256], P(('row', 'col')), may hold values from -6 to 6
- tile_vals: float32 [4, 8, 4, 128, 128], P('row', 'col'), may hold values from -0.1875 to 0.1875
- tile_ids: int32 [4, 8, 4], P('row', 'col'), may hold values from 0 to 7, as said below
- tile_count: int32 [4, 8], P('row', 'col'), may hold values from 2 to 4, as said below
- weight: float32 [256, 256], replicated, may hold values from -0.375 to 0.375
Outputs:
- activations: float32 [8, 256, 256], P('col', 'row')
The draws below stay inside these ranges and needn't reach their ends.
Inputs may be any that keep to these rules, and one draw needn't show every extreme that they name: `tile_ids`: the first tile_count entries of a region's list name distinct tiles; later entries are unused. `tile_count`: some region lists 4 tiles in every draw.
All inputs are finite; a program needn't handle non-finite values.
Results may differ from the reference program's by a relative error of at most 0.0003.
Values sent between devices are 32-bit elements; how exact they have to be, the bound alone decides.
A program may use at most 64 MiB of HBM per device.

```python
import jax
import jax.numpy as jnp
from jax import lax

F = 256
TILE = 128
N = 2048
OUTB = 256
INB = 512
ROW_TILES = 2
COL_TILES = 4
CAP = 4
N_ROW = 4
N_COL = 8


def draw_tile_ids(key, part):
    regions = N_ROW * N_COL
    keys = jax.random.split(jax.random.fold_in(key, 11), regions)
    orders = jax.vmap(lambda single: jax.random.permutation(single, ROW_TILES * COL_TILES))(keys)
    return orders[:, :CAP].reshape(N_ROW, N_COL, CAP).astype(jnp.int32)


def draw_tile_count(key, part):
    regions = N_ROW * N_COL
    counts = jax.random.randint(jax.random.fold_in(key, 23), (regions,), CAP // 2, CAP + 1)
    fullest = jax.random.randint(jax.random.fold_in(key, 29), (), 0, regions)
    counts = counts.at[fullest].set(CAP)
    return counts.reshape(N_ROW, N_COL).astype(jnp.int32)


def block_scale(own_key, extent, shards, low, top_value):
    def one(position, parts):
        draws = jax.random.uniform(jax.random.fold_in(jax.random.fold_in(own_key, 6), position), (parts,), jnp.float32, low / len(shards), top_value / len(shards))
        return jnp.repeat(jnp.exp(draws), extent[position] // parts).reshape((-1,) + (1,) * (len(extent) - position - 1))

    factor_of = one(*shards[0])
    for cut in shards[1:]:
        factor_of = factor_of * one(*cut)
    return factor_of


def gaussian(own_key, dims, deviation, bound, shards=(), dtype=jnp.bfloat16):
    entries = deviation * jax.random.normal(own_key, dims, jnp.float32)
    if shards:
        entries = entries * block_scale(own_key, dims, shards, -0.22, 0.18)
    return jnp.clip(entries, -bound, bound).astype(dtype)


def setup_inputs(seed: int = 0) -> dict:
    streams_of = jax.random.split(jax.random.key(seed), 6)
    return {
        "features": gaussian(streams_of[0], (N, F), 1.0, 6.0, ((0, 32),), jnp.float32),
        "tile_vals": gaussian(streams_of[1], (N_ROW, N_COL, CAP, TILE, TILE), (N_ROW * CAP * TILE // ROW_TILES) ** -0.5, 0.1875, ((0, 4), (1, 8)), jnp.float32),
        "tile_ids": draw_tile_ids(jax.random.fold_in(streams_of[5], 71), 0),
        "tile_count": draw_tile_count(jax.random.fold_in(streams_of[5], 71), 0),
        "weight": gaussian(streams_of[4], (F, F), F ** -0.5, 0.375, (), jnp.float32),
    }


def region_sum(region_vals, region_ids, region_count, source):
    col_tiles = source.shape[0] // TILE
    picked = source.reshape(col_tiles, TILE, source.shape[1])[region_ids % col_tiles]
    products = jnp.einsum("kab,kbf->kaf", region_vals, picked, precision=lax.Precision.HIGHEST)
    listed = jnp.arange(region_vals.shape[0]) < region_count
    row_tile = region_ids // col_tiles
    one_hot = ((row_tile[:, None] == jnp.arange(ROW_TILES)[None, :]) & listed[:, None]).astype(jnp.float32)
    return jnp.einsum("kr,kaf->raf", one_hot, products, precision=lax.Precision.HIGHEST)


def reference(features, tile_vals, tile_ids, tile_count, weight):
    groups = features.reshape(N_ROW, INB, F)

    def per_block(col_index):
        def per_group(running, row_index):
            region = region_sum(tile_vals[row_index, col_index], tile_ids[row_index, col_index], tile_count[row_index, col_index], groups[row_index])
            return running + region, None

        start = jnp.zeros((ROW_TILES, TILE, F), jnp.float32)
        total, unused = lax.scan(per_group, start, jnp.arange(N_ROW))
        return total.reshape(OUTB, F)

    aggregate = lax.map(per_block, jnp.arange(N_COL))
    mixed = jnp.einsum("cvf,fg->cvg", aggregate, weight, precision=lax.Precision.HIGHEST)
    return jnp.maximum(mixed, 0.0)
```

```python
import functools

import jax
import jax.numpy as jnp
from jax import lax
from jax.experimental import pallas as pl
from jax.experimental.pallas import tpu as pltpu
from jax.sharding import PartitionSpec as P

LANES = 256
MESH = pl.DeviceIdType.MESH


def split(x):
    high = x.astype(jnp.bfloat16)
    low = (x - high.astype(jnp.float32)).astype(jnp.bfloat16)
    return high, low


def dot3(a_high, a_low, b_high, b_low):
    mul = functools.partial(jnp.dot, preferred_element_type=jnp.float32)
    return mul(a_high, b_high) + (mul(a_low, b_high) + mul(a_high, b_low))


def flip(index, bits):
    bit = 1
    while bit <= bits:
        if bits & bit:
            index = index + bit * (1 - 2 * (index // bit % 2))
        bit *= 2
    return index


def loop(count, body):
    if count <= 8:
        for i in range(count):
            body(i)
    else:
        lax.fori_loop(0, count, lambda i, c: (body(i), c)[1], 0)


def kernel(
    rows, cols,
    feat_ref, vals_ref, ids_hbm, count_hbm, weight_ref, out_ref, ids_ref, count_ref,
    xbuf, vals, weight, adj, wsplit, part, landed,
    local_sem, send_own, send_par, send_rel, recv_ring, recv_par, send_rs, recv_rs, ready,
):
    me_row, me_col = lax.axis_index("row"), lax.axis_index("col")
    chips = cols // 2
    chip, core = me_col // 2, me_col % 2
    piece = feat_ref.shape[0]
    chunks = feat_ref.shape[1] // LANES
    slots, tile = vals.shape[0], vals.shape[1]
    col_tiles = cols * piece // tile
    row_tiles = rows * piece // tile
    upward = [d for d in (1, 2) if d < chips]
    downward = list(range(1 - chips, 0))

    def inside(d):
        return jnp.logical_and(chip + d >= 0, chip + d < chips)

    load_own = [
        pltpu.make_async_copy(
            feat_ref.at[:, pl.ds(h * LANES, LANES)], xbuf.at[h, me_col], local_sem.at[2 + h]
        )
        for h in range(chunks)
    ]
    load_vals = pltpu.make_async_copy(vals_ref.at[0, 0], vals, local_sem.at[0])
    load_weight = pltpu.make_async_copy(weight_ref, weight, local_sem.at[1])
    load_ids = pltpu.make_async_copy(ids_hbm, ids_ref, local_sem.at[2 + chunks])
    load_count = pltpu.make_async_copy(count_hbm, count_ref, local_sem.at[3 + chunks])
    load_ids.start()
    load_count.start()
    load_vals.start()
    load_weight.start()
    for copy in load_own:
        copy.start()

    barrier = pltpu.get_barrier_semaphore()
    expected = jnp.int32(rows)
    for s in range(1, rows):
        pl.semaphore_signal(
            barrier, inc=1, device_id=(lax.rem(me_row + s, rows), me_col), device_id_type=MESH
        )
    pl.semaphore_signal(barrier, inc=1, device_id=(me_row, chip * 2 + 1 - core), device_id_type=MESH)
    for d in range(1, chips):
        expected = expected + inside(-d).astype(jnp.int32)

        @pl.when(inside(d))
        def _(d=d):
            pl.semaphore_signal(barrier, inc=1, device_id=(me_row, me_col + 2 * d), device_id_type=MESH)

    pl.semaphore_wait(barrier, expected)

    def own(h):
        return feat_ref.at[:, pl.ds(h * LANES, LANES)]

    def own_send(h, n, d):
        return pltpu.make_async_remote_copy(
            src_ref=own(h), dst_ref=xbuf.at[h, me_col],
            send_sem=send_own.at[h, n], recv_sem=recv_ring.at[h, chip],
            device_id=(me_row, me_col + 2 * d), device_id_type=MESH,
        )

    def partner_own(h):
        return pltpu.make_async_remote_copy(
            src_ref=own(h), dst_ref=xbuf.at[h, me_col],
            send_sem=send_par.at[h, chip], recv_sem=recv_par.at[h, chip],
            device_id=(me_row, chip * 2 + 1 - core), device_id_type=MESH,
        )

    def partner_pass(h, p):
        return pltpu.make_async_remote_copy(
            src_ref=xbuf.at[h, 2 * p + core], dst_ref=xbuf.at[h, 2 * p + core],
            send_sem=send_par.at[h, p], recv_sem=recv_par.at[h, p],
            device_id=(me_row, chip * 2 + 1 - core), device_id_type=MESH,
        )

    def relay(h, p, step):
        return pltpu.make_async_remote_copy(
            src_ref=xbuf.at[h, 2 * p + core], dst_ref=xbuf.at[h, 2 * p + core],
            send_sem=send_rel.at[h, p], recv_sem=recv_ring.at[h, p],
            device_id=(me_row, me_col + 2 * step), device_id_type=MESH,
        )

    def from_partner(h, p):
        return pltpu.make_async_remote_copy(
            src_ref=xbuf.at[h, 2 * p + 1 - core], dst_ref=xbuf.at[h, 2 * p + 1 - core],
            send_sem=send_par.at[h, p], recv_sem=recv_par.at[h, p],
            device_id=(me_row, chip * 2 + 1 - core), device_id_type=MESH,
        )

    def scatter(h, s):
        owner = flip(me_row, s)
        return pltpu.make_async_remote_copy(
            src_ref=part.at[h, pl.ds(owner * piece, piece)], dst_ref=landed.at[h, s - 1],
            send_sem=send_rs.at[h, s - 1], recv_sem=recv_rs.at[h, s - 1],
            device_id=(owner, me_col), device_id_type=MESH,
        )

    for n, d in enumerate(upward):

        @pl.when(inside(-d))
        def _(n=n, d=d):
            pl.semaphore_signal(
                ready.at[n], inc=1, device_id=(me_row, me_col - 2 * d), device_id_type=MESH
            )

    for n, d in enumerate(downward):
        for h in range(chunks):
            pl.when(inside(d))(own_send(h, len(upward) + n, d).start)
    for h in range(chunks):
        partner_own(h).start()

    def send_up(n, d):
        @pl.when(inside(d))
        def _():
            pl.semaphore_wait(ready.at[n], 1)
            for h in range(chunks):
                own_send(h, n, d).start()

    for n, d in enumerate(upward[:1]):
        send_up(n, d)
    load_ids.wait()
    load_count.wait()
    load_vals.wait()

    def place(t):
        found = jnp.int32(0)
        slot = jnp.int32(0)

        def look(k, carry):
            hit = jnp.logical_and(ids_ref[0, 0, k] == t, k < count_ref[0, 0])
            return jnp.where(hit, 1, carry[0]), jnp.where(hit, k, carry[1])

        found, slot = lax.fori_loop(0, slots, look, (found, slot), unroll=slots <= 8)
        high, low = split(jnp.where(found == 1, vals[slot], 0.0))
        at = (pl.ds((t // col_tiles) * tile, tile), pl.ds((t % col_tiles) * tile, tile))
        adj[(0,) + at] = high
        adj[(1,) + at] = low

    loop(row_tiles * col_tiles, place)

    load_weight.wait()
    high, low = split(weight[...])
    wsplit[0] = high
    wsplit[1] = low

    for n, d in enumerate(upward[1:], 1):
        send_up(n, d)

    block = min(256, rows * piece)
    for h in range(chunks):
        for step in (1, -1):
            for d in range(1, chips):
                p = chip - step * d

                @pl.when(inside(-step * d))
                def _(h=h, d=d, step=step, p=p):
                    relay(h, p, step).wait_recv()
                    if d >= 2 and step == 1:
                        pl.when(inside(step))(relay(h, p, step).start)
                    partner_pass(h, p).start()

        load_own[h].wait()
        for p in range(chips):
            from_partner(h, p).wait_recv()

        x_high, x_low = split(xbuf[h].reshape(cols * piece, LANES))

        def product(b):
            at = pl.ds(b * block, block)
            part[h, at, :] = dot3(adj[0, at, :], adj[1, at, :], x_high, x_low)

        loop(rows * piece // block, product)
        for s in reversed(range(1, rows)):
            scatter(h, s).start()

    mixed = jnp.zeros((piece, weight.shape[1]), jnp.float32)
    for h in range(chunks):
        owned = part[h, pl.ds(me_row * piece, piece), :]
        for s in range(1, rows):
            scatter(h, s).wait_recv()
            owned = owned + landed[h, s - 1]
        o_high, o_low = split(owned)
        at = pl.ds(h * LANES, LANES)
        mixed = mixed + dot3(o_high, o_low, wsplit[0, at, :], wsplit[1, at, :])
    out_ref[...] = jnp.maximum(mixed, 0.0)

    for h in range(chunks):
        for n, d in enumerate(upward + downward):
            pl.when(inside(d))(own_send(h, n, d).wait_send)
        partner_own(h).wait_send()
        for d in range(1, chips):
            for step in (1, -1):
                p = chip - step * d

                @pl.when(inside(-step * d))
                def _(h=h, d=d, step=step, p=p):
                    partner_pass(h, p).wait_send()
                    if d >= 2 and step == 1:
                        pl.when(inside(step))(relay(h, p, step).wait_send)

        for s in range(1, rows):
            scatter(h, s).wait_send()


def local(rows, cols, features, tile_vals, tile_ids, tile_count, weight):
    piece, width = features.shape
    chunks = width // LANES
    chips = cols // 2
    slots, tile = tile_vals.shape[2], tile_vals.shape[3]
    f32, bf16 = jnp.float32, jnp.bfloat16
    dma = pltpu.SemaphoreType.DMA
    out = pl.pallas_call(
        functools.partial(kernel, rows, cols),
        out_shape=pltpu.VMEM((piece, weight.shape[1]), f32),
        in_specs=[
            pl.BlockSpec(memory_space=pl.ANY),
            pl.BlockSpec(memory_space=pl.ANY),
            pl.BlockSpec(memory_space=pl.ANY),
            pl.BlockSpec(memory_space=pl.ANY),
            pl.BlockSpec(memory_space=pl.ANY),
        ],
        out_specs=pl.BlockSpec(memory_space=pltpu.VMEM),
        scratch_shapes=[
            pltpu.SMEM(tile_ids.shape, jnp.int32),
            pltpu.SMEM(tile_count.shape, jnp.int32),
            pltpu.VMEM((chunks, cols, piece, LANES), f32),
            pltpu.VMEM((slots, tile, tile), f32),
            pltpu.VMEM(weight.shape, f32),
            pltpu.VMEM((2, rows * piece, cols * piece), bf16),
            pltpu.VMEM((2,) + weight.shape, bf16),
            pltpu.VMEM((chunks, rows * piece, LANES), f32),
            pltpu.VMEM((chunks, rows - 1, piece, LANES), f32),
            dma((4 + chunks,)),
            dma((chunks, 2 + chips)),
            dma((chunks, chips)),
            dma((chunks, chips)),
            dma((chunks, chips)),
            dma((chunks, chips)),
            dma((chunks, rows - 1)),
            dma((chunks, rows - 1)),
            pltpu.SemaphoreType.REGULAR((2,)),
        ],
        compiler_params=pltpu.CompilerParams(collective_id=0, has_side_effects=True),
    )(features, tile_vals, tile_ids, tile_count, weight)
    return out.reshape(1, piece, weight.shape[1])


def solution(mesh):
    in_specs = (
        P(("row", "col"), None),
        P("row", "col", None, None, None),
        P("row", "col", None),
        P("row", "col"),
        P(),
    )
    body = functools.partial(local, mesh.shape["row"], mesh.shape["col"])
    return jax.shard_map(
        body, mesh=mesh, in_specs=in_specs, out_specs=P("col", "row", None), check_vma=False
    )
```

```python
import functools

import jax
import jax.numpy as jnp
from jax import lax
from jax.experimental import pallas as pl
from jax.experimental.pallas import tpu as pltpu
from jax.sharding import PartitionSpec as P

LANES = 256
MESH = pl.DeviceIdType.MESH


def split(x):
    high = x.astype(jnp.bfloat16)
    low = (x - high.astype(jnp.float32)).astype(jnp.bfloat16)
    return high, low


def dot3(a_high, a_low, b_high, b_low):
    mul = functools.partial(jnp.dot, preferred_element_type=jnp.float32)
    return mul(a_high, b_high) + (mul(a_low, b_high) + mul(a_high, b_low))


def flip(index, bits):
    bit = 1
    while bit <= bits:
        if bits & bit:
            index = index + bit * (1 - 2 * (index // bit % 2))
        bit *= 2
    return index


def loop(count, body):
    if count <= 8:
        for i in range(count):
            body(i)
    else:
        lax.fori_loop(0, count, lambda i, c: (body(i), c)[1], 0)


def kernel(
    rows, cols,
    feat_ref, vals_ref, ids_hbm, count_hbm, weight_ref, out_ref, ids_ref, count_ref,
    xbuf, vals, weight, adj, wsplit, part, landed,
    local_sem, send_own, send_par, send_rel, recv_ring, recv_par, send_rs, recv_rs, ready, ready_row, ready_par,
):
    me_row, me_col = lax.axis_index("row"), lax.axis_index("col")
    chips = cols // 2
    chip, core = me_col // 2, me_col % 2
    piece = feat_ref.shape[0]
    chunks = feat_ref.shape[1] // LANES
    slots, tile = vals.shape[0], vals.shape[1]
    col_tiles = cols * piece // tile
    row_tiles = rows * piece // tile
    upward = [d for d in (1, 2) if d < chips]
    downward = list(range(1 - chips, 0))

    def inside(d):
        return jnp.logical_and(chip + d >= 0, chip + d < chips)

    load_own = [
        pltpu.make_async_copy(
            feat_ref.at[:, pl.ds(h * LANES, LANES)], xbuf.at[h, me_col], local_sem.at[2 + h]
        )
        for h in range(chunks)
    ]
    load_vals = pltpu.make_async_copy(vals_ref.at[0, 0], vals, local_sem.at[0])
    load_weight = pltpu.make_async_copy(weight_ref, weight, local_sem.at[1])
    load_ids = pltpu.make_async_copy(ids_hbm, ids_ref, local_sem.at[2 + chunks])
    load_count = pltpu.make_async_copy(count_hbm, count_ref, local_sem.at[3 + chunks])
    load_ids.start()
    load_count.start()
    load_vals.start()
    load_weight.start()
    for copy in load_own:
        copy.start()

    barrier = pltpu.get_barrier_semaphore()
    partner = chip * 2 + 1 - core
    expected = me_row + core
    for s in range(1, rows):

        @pl.when(me_row + s < rows)
        def _(s=s):
            pl.semaphore_signal(barrier, inc=1, device_id=(me_row + s, me_col), device_id_type=MESH)

    @pl.when(core == 0)
    def _():
        pl.semaphore_signal(barrier, inc=1, device_id=(me_row, partner), device_id_type=MESH)

    for d in range(1, chips):
        expected = expected + inside(-d).astype(jnp.int32)

        @pl.when(inside(d))
        def _(d=d):
            pl.semaphore_signal(barrier, inc=1, device_id=(me_row, me_col + 2 * d), device_id_type=MESH)

    @pl.when(expected > 0)
    def _():
        pl.semaphore_wait(barrier, expected)

    def own(h):
        return feat_ref.at[:, pl.ds(h * LANES, LANES)]

    def own_send(h, n, d):
        return pltpu.make_async_remote_copy(
            src_ref=own(h), dst_ref=xbuf.at[h, me_col],
            send_sem=send_own.at[h, n], recv_sem=recv_ring.at[h, chip],
            device_id=(me_row, me_col + 2 * d), device_id_type=MESH,
        )

    def partner_own(h):
        return pltpu.make_async_remote_copy(
            src_ref=own(h), dst_ref=xbuf.at[h, me_col],
            send_sem=send_par.at[h, chip], recv_sem=recv_par.at[h, chip],
            device_id=(me_row, chip * 2 + 1 - core), device_id_type=MESH,
        )

    def partner_pass(h, p):
        return pltpu.make_async_remote_copy(
            src_ref=xbuf.at[h, 2 * p + core], dst_ref=xbuf.at[h, 2 * p + core],
            send_sem=send_par.at[h, p], recv_sem=recv_par.at[h, p],
            device_id=(me_row, chip * 2 + 1 - core), device_id_type=MESH,
        )

    def relay(h, p, step):
        return pltpu.make_async_remote_copy(
            src_ref=xbuf.at[h, 2 * p + core], dst_ref=xbuf.at[h, 2 * p + core],
            send_sem=send_rel.at[h, p], recv_sem=recv_ring.at[h, p],
            device_id=(me_row, me_col + 2 * step), device_id_type=MESH,
        )

    def from_partner(h, p):
        return pltpu.make_async_remote_copy(
            src_ref=xbuf.at[h, 2 * p + 1 - core], dst_ref=xbuf.at[h, 2 * p + 1 - core],
            send_sem=send_par.at[h, p], recv_sem=recv_par.at[h, p],
            device_id=(me_row, chip * 2 + 1 - core), device_id_type=MESH,
        )

    def scatter(h, s):
        owner = flip(me_row, s)
        return pltpu.make_async_remote_copy(
            src_ref=part.at[h, pl.ds(owner * piece, piece)], dst_ref=landed.at[h, s - 1],
            send_sem=send_rs.at[h, s - 1], recv_sem=recv_rs.at[h, s - 1],
            device_id=(owner, me_col), device_id_type=MESH,
        )

    for n, d in enumerate(upward):

        @pl.when(inside(-d))
        def _(n=n, d=d):
            pl.semaphore_signal(
                ready.at[n], inc=1, device_id=(me_row, me_col - 2 * d), device_id_type=MESH
            )

    for n, d in enumerate(downward):
        for h in range(chunks):
            pl.when(inside(d))(own_send(h, len(upward) + n, d).start)

    @pl.when(core == 1)
    def _():
        pl.semaphore_signal(ready_par, inc=1, device_id=(me_row, partner), device_id_type=MESH)

    for s in range(1, rows):

        @pl.when(flip(me_row, s) < me_row)
        def _(s=s):
            pl.semaphore_signal(
                ready_row.at[s - 1], inc=1, device_id=(flip(me_row, s), me_col), device_id_type=MESH
            )

    @pl.when(core == 0)
    def _():
        pl.semaphore_wait(ready_par, 1)

    for h in range(chunks):
        partner_own(h).start()

    def send_up(n, d):
        @pl.when(inside(d))
        def _():
            pl.semaphore_wait(ready.at[n], 1)
            for h in range(chunks):
                own_send(h, n, d).start()

    for n, d in enumerate(upward[:1]):
        send_up(n, d)
    load_ids.wait()
    load_count.wait()
    load_vals.wait()

    def place(t):
        found = jnp.int32(0)
        slot = jnp.int32(0)

        def look(k, carry):
            hit = jnp.logical_and(ids_ref[0, 0, k] == t, k < count_ref[0, 0])
            return jnp.where(hit, 1, carry[0]), jnp.where(hit, k, carry[1])

        found, slot = lax.fori_loop(0, slots, look, (found, slot), unroll=slots <= 8)
        high, low = split(jnp.where(found == 1, vals[slot], 0.0))
        at = (pl.ds((t // col_tiles) * tile, tile), pl.ds((t % col_tiles) * tile, tile))
        adj[(0,) + at] = high
        adj[(1,) + at] = low

    loop(row_tiles * col_tiles, place)

    load_weight.wait()
    high, low = split(weight[...])
    wsplit[0] = high
    wsplit[1] = low

    for n, d in enumerate(upward[1:], 1):
        send_up(n, d)

    block = min(256, rows * piece)
    for h in range(chunks):
        for step in (1, -1):
            for d in range(1, chips):
                p = chip - step * d

                @pl.when(inside(-step * d))
                def _(h=h, d=d, step=step, p=p):
                    relay(h, p, step).wait_recv()
                    if d >= 2 and step == 1:
                        pl.when(inside(step))(relay(h, p, step).start)
                    partner_pass(h, p).start()

        load_own[h].wait()
        for p in range(chips):
            from_partner(h, p).wait_recv()

        x_high, x_low = split(xbuf[h].reshape(cols * piece, LANES))

        def product(b):
            at = pl.ds(b * block, block)
            part[h, at, :] = dot3(adj[0, at, :], adj[1, at, :], x_high, x_low)

        loop(rows * piece // block, product)
        for s in reversed(range(1, rows)):
            if h == 0:

                @pl.when(flip(me_row, s) > me_row)
                def _(s=s):
                    pl.semaphore_wait(ready_row.at[s - 1], 1)

            scatter(h, s).start()

    mixed = jnp.zeros((piece, weight.shape[1]), jnp.float32)
    for h in range(chunks):
        owned = part[h, pl.ds(me_row * piece, piece), :]
        for s in range(1, rows):
            scatter(h, s).wait_recv()
            owned = owned + landed[h, s - 1]
        o_high, o_low = split(owned)
        at = pl.ds(h * LANES, LANES)
        mixed = mixed + dot3(o_high, o_low, wsplit[0, at, :], wsplit[1, at, :])
    out_ref[...] = jnp.maximum(mixed, 0.0)

    for h in range(chunks):
        for n, d in enumerate(upward + downward):
            pl.when(inside(d))(own_send(h, n, d).wait_send)
        partner_own(h).wait_send()
        for d in range(1, chips):
            for step in (1, -1):
                p = chip - step * d

                @pl.when(inside(-step * d))
                def _(h=h, d=d, step=step, p=p):
                    partner_pass(h, p).wait_send()
                    if d >= 2 and step == 1:
                        pl.when(inside(step))(relay(h, p, step).wait_send)

        for s in range(1, rows):
            scatter(h, s).wait_send()


def local(rows, cols, features, tile_vals, tile_ids, tile_count, weight):
    piece, width = features.shape
    chunks = width // LANES
    chips = cols // 2
    slots, tile = tile_vals.shape[2], tile_vals.shape[3]
    f32, bf16 = jnp.float32, jnp.bfloat16
    dma = pltpu.SemaphoreType.DMA
    out = pl.pallas_call(
        functools.partial(kernel, rows, cols),
        out_shape=pltpu.VMEM((piece, weight.shape[1]), f32),
        in_specs=[
            pl.BlockSpec(memory_space=pl.ANY),
            pl.BlockSpec(memory_space=pl.ANY),
            pl.BlockSpec(memory_space=pl.ANY),
            pl.BlockSpec(memory_space=pl.ANY),
            pl.BlockSpec(memory_space=pl.ANY),
        ],
        out_specs=pl.BlockSpec(memory_space=pltpu.VMEM),
        scratch_shapes=[
            pltpu.SMEM(tile_ids.shape, jnp.int32),
            pltpu.SMEM(tile_count.shape, jnp.int32),
            pltpu.VMEM((chunks, cols, piece, LANES), f32),
            pltpu.VMEM((slots, tile, tile), f32),
            pltpu.VMEM(weight.shape, f32),
            pltpu.VMEM((2, rows * piece, cols * piece), bf16),
            pltpu.VMEM((2,) + weight.shape, bf16),
            pltpu.VMEM((chunks, rows * piece, LANES), f32),
            pltpu.VMEM((chunks, rows - 1, piece, LANES), f32),
            dma((4 + chunks,)),
            dma((chunks, 2 + chips)),
            dma((chunks, chips)),
            dma((chunks, chips)),
            dma((chunks, chips)),
            dma((chunks, chips)),
            dma((chunks, rows - 1)),
            dma((chunks, rows - 1)),
            pltpu.SemaphoreType.REGULAR((2,)),
            pltpu.SemaphoreType.REGULAR((rows - 1,)),
            pltpu.SemaphoreType.REGULAR,
        ],
        compiler_params=pltpu.CompilerParams(collective_id=0, has_side_effects=True),
    )(features, tile_vals, tile_ids, tile_count, weight)
    return out.reshape(1, piece, weight.shape[1])


def solution(mesh):
    in_specs = (
        P(("row", "col"), None),
        P("row", "col", None, None, None),
        P("row", "col", None),
        P("row", "col"),
        P(),
    )
    body = functools.partial(local, mesh.shape["row"], mesh.shape["col"])
    return jax.shard_map(
        body, mesh=mesh, in_specs=in_specs, out_specs=P("col", "row", None), check_vma=False
    )
```
